256 devices in a mesh: prow: 16 (over z, core), pcol: 16 (over x, y).
Axes of the slice: x: 4, y: 4, z: 8, core: 2. Of those that a mesh axis runs over, the one named last changes fastest.
Arguments:
- tiles: bfloat16 [32768, 128, 128], P(('prow', 'pcol')), may hold values from -6 to 6
- tile_pos: int32 [32768, 2], P(('prow', 'pcol')), may hold values from -1 to 511, as said below
- pivots: int32 [2, 256], replicated, may hold values from 0 to 255, each once within a row
- inverses: bfloat16 [2, 256, 256], replicated, may hold values from -0.0234375 to 0.0234375
Outputs:
- factored: bfloat16 [32768, 128, 128], P(('prow', 'pcol'))
The draws below stay inside these ranges and needn't reach their ends.
Inputs may be any that keep to these rules, and one draw needn't show every extreme that they name: `tile_pos`: slot s of device (p, q) (device index p * 16 + q, p along prow) holds a tile (I, J) with I % 16 == p and (J // 2) % 16 == q, or is empty; no tile is listed twice; every tile with I < 4 or J < 4 is listed; listed slots come before empty ones on each device; some device has all 128 slots listed.
All inputs are finite; a program needn't handle non-finite values.
Results may differ from the reference program's by a relative error of at most 0.0067.
Values may be sent and summed in bfloat16 or wider, within the bound.
No kernel may reach another device: no remote copies, remote signals or barrier semaphores. Data moves between devices by JAX's collectives and lax.ppermute only.
A program may use at most 128 MiB of HBM per device.

```python
import math
import jax
import jax.numpy as jnp
from jax import lax

TILE = 128
PANEL = 256
ROW_TILES = 32
PAIRS = 16
SLOTS = 128
ORDER = 65536
N_PROW = 16
N_PCOL = 16


def draw_tile_pos(key, part):
    row_procs = N_PROW
    col_procs = N_PCOL
    count = row_procs * col_procs
    col_tiles = 2 * PAIRS
    cells = ROW_TILES * col_tiles
    device = jnp.arange(count, dtype=jnp.int32)
    proc_row = (device // col_procs)[:, None, None]
    proc_col = (device % col_procs)[:, None, None]
    local_i = jnp.arange(ROW_TILES, dtype=jnp.int32)[None, :, None]
    local_q = jnp.arange(col_tiles, dtype=jnp.int32)[None, None, :]
    glob_row = jnp.broadcast_to(proc_row + row_procs * local_i, (count, ROW_TILES, col_tiles)).reshape(count, cells)
    glob_col = jnp.broadcast_to(2 * (proc_col + col_procs * (local_q // 2)) + local_q % 2, (count, ROW_TILES, col_tiles)).reshape(count, cells)
    dense = (glob_row < 4) | (glob_col < 4)
    keys = jax.random.split(jax.random.fold_in(key, 11), count)
    ranks = jax.vmap(lambda k: jax.random.permutation(k, cells))(keys).astype(jnp.int32)
    priority = jnp.where(dense, -1, ranks)
    order = jnp.argsort(priority, axis=1, stable=True)[:, :SLOTS]
    dense_count = jnp.sum(dense.astype(jnp.int32), axis=1)
    room = SLOTS - dense_count
    extra = jax.random.randint(jax.random.fold_in(key, 12), (count,), 0, room + 1)
    chosen = jax.random.randint(jax.random.fold_in(key, 13), (), 0, count)
    extra = jnp.where(device == chosen, room, extra)
    live = jnp.arange(SLOTS, dtype=jnp.int32)[None, :] < (dense_count + extra)[:, None]
    rows = jnp.take_along_axis(glob_row, order, axis=1)
    cols = jnp.take_along_axis(glob_col, order, axis=1)
    rows = jnp.where(live, rows, -1)
    cols = jnp.where(live, cols, -1)
    return jnp.stack([rows, cols], axis=-1).reshape(count * SLOTS, 2).astype(jnp.int32)


def shard_levels(own_key, dims, pieces, least, largest):
    loudness = 1.0
    for axis_at, blocks in pieces:
        draws = jax.random.uniform(jax.random.fold_in(jax.random.fold_in(own_key, 6), axis_at), (blocks,), jnp.float32, least / len(pieces), largest / len(pieces))
        loudness = loudness * jnp.repeat(jnp.exp(draws), dims[axis_at] // blocks).reshape((-1,) + (1,) * (len(dims) - 1 - axis_at))
    return loudness


def centred(stream_key, shape, width, reach, cuts=(), kind=jnp.bfloat16):
    entries = jax.random.normal(stream_key, shape, jnp.float32) * width
    if len(cuts) > 0:
        entries = shard_levels(stream_key, shape, cuts, -0.22, 0.18) * entries
    return jnp.clip(entries, min=-reach, max=reach).astype(kind)


def setup_inputs(seed: int = 0) -> dict:
    key_list = jax.random.split(jax.random.key(seed), 5)
    tiles = centred(key_list[0], (N_PROW * N_PCOL * SLOTS, TILE, TILE), 1.0, 6.0, ((0, 256),))
    tile_pos = draw_tile_pos(jax.random.fold_in(key_list[4], 71), 0)
    pivots = jax.vmap(lambda own: jax.random.permutation(own, PANEL))(jax.random.split(key_list[2], 2)).reshape((2, PANEL)).astype(jnp.int32)
    inverses = centred(key_list[3], (2, PANEL, PANEL), (PANEL * PANEL) ** -0.5, 0.0234375)
    return {"tiles": tiles, "tile_pos": tile_pos, "pivots": pivots, "inverses": inverses}


def panel_step(current, tile_row, tile_col, order, inverse, first, tiles_n):
    edge = current.shape[1]
    in_column = (tile_col >= first) & (tile_col < first + 2)
    col_keys = jnp.where(in_column, tile_row * 2 + tile_col - first, 2 * tiles_n).astype(jnp.int32)
    column = jnp.zeros((2 * tiles_n, edge, edge), current.dtype).at[col_keys].set(current, mode="drop")
    column = column.reshape(tiles_n, 2, edge, edge).transpose(0, 2, 1, 3).reshape(tiles_n * edge, 2 * edge)
    lower = jnp.dot(column, inverse, preferred_element_type=jnp.float32).astype(jnp.bfloat16)
    in_block = (tile_row >= first) & (tile_row < first + 2)
    row_keys = jnp.where(in_block, (tile_row - first) * tiles_n + tile_col, 2 * tiles_n).astype(jnp.int32)
    rows = jnp.zeros((2 * tiles_n, edge, edge), current.dtype).at[row_keys].set(current, mode="drop")
    rows = rows.reshape(2, tiles_n, edge, edge).transpose(0, 2, 1, 3).reshape(2 * edge, tiles_n * edge)
    upper = rows[order]
    lower_tiles = lower.reshape(tiles_n, edge, 2 * edge)
    upper_tiles = upper.reshape(2 * edge, tiles_n, edge).transpose(1, 0, 2)
    lower_parts = lower_tiles.reshape(tiles_n, edge, 2, edge).transpose(0, 2, 1, 3)
    upper_parts = upper_tiles.reshape(tiles_n, 2, edge, edge)
    total = current.shape[0]
    blk = math.gcd(total, 256)
    count = total // blk

    def one_block(args):
        cur, rws, cls = args
        safe_row = jnp.clip(rws, 0, tiles_n - 1)
        safe_col = jnp.clip(cls, 0, tiles_n - 1)
        left = lower_tiles[safe_row].astype(jnp.float32)
        right = upper_tiles[safe_col].astype(jnp.float32)
        product = jnp.einsum("sik,skj->sij", left, right, precision=lax.Precision.HIGHEST)
        updated = (cur.astype(jnp.float32) - product).astype(jnp.bfloat16)
        trailing = (rws >= first + 2) & (cls >= first + 2)
        is_lower = (cls >= first) & (cls < first + 2) & (rws >= first + 2)
        is_upper = (rws >= first) & (rws < first + 2)
        lower_write = lower_parts[safe_row, jnp.clip(cls - first, 0, 1)]
        upper_write = upper_parts[safe_col, jnp.clip(rws - first, 0, 1)]
        out = jnp.where(trailing[:, None, None], updated, cur)
        out = jnp.where(is_lower[:, None, None], lower_write, out)
        out = jnp.where(is_upper[:, None, None], upper_write, out)
        return out

    result = lax.map(one_block, (current.reshape(count, blk, edge, edge), tile_row.reshape(count, blk), tile_col.reshape(count, blk)))
    return result.reshape(current.shape)


def reference(tiles, tile_pos, pivots, inverses):
    tiles_n = ORDER // TILE
    tile_row = tile_pos[:, 0]
    tile_col = tile_pos[:, 1]
    current = tiles
    for panel in range(2):
        current = panel_step(current, tile_row, tile_col, pivots[panel], inverses[panel], 2 * panel, tiles_n)
    return current
```

```python
import functools

import jax
import jax.numpy as jnp
from jax import lax
from jax.experimental import pallas as pl
from jax.experimental.pallas import tpu as pltpu
from jax.sharding import PartitionSpec as P

T = 128
BF = jnp.bfloat16
F32 = jnp.float32
SLOTS = 128
ROWS = 32
COLS = 32


ALONG_Y = [[x * 4 + y for y in range(4)] for x in range(4)]
SAME_CORE = [[z * 2 + c for z in range(8)] for c in range(2)]
SWAP = [(p, p ^ 1) for p in range(16)]
UP_Z = [(p, (p + 2) % 16) for p in range(16)]


def move_x(d):
    return [(x * 4 + y, (x + d) % 4 * 4 + y) for x in range(4) for y in range(4)]


def move_y(d):
    return [(x * 4 + y, x * 4 + (y + d) % 4) for x in range(4) for y in range(4)]


def scatter_z(m):
    return [(k * 2 + c, (2 * m + k) * 2 + c) for k in range(2) for c in range(2)]


VM = pl.BlockSpec(memory_space=pltpu.VMEM)
SM = pl.BlockSpec(memory_space=pltpu.SMEM)


def extract_columns_kernel(pos, tiles, col):
    @pl.loop(0, SLOTS)
    def _(s):
        i = pos[0, s]
        j = pos[1, s]

        @pl.when((j >= 0) & (j < 4))
        def _():
            col[(i // 16) * 2 + j % 2] = tiles[s]


def extract_rows_kernel(pos, tiles, after, *quarters):
    @pl.loop(0, SLOTS)
    def _(s):
        i = pos[0, s]
        j = pos[1, s]

        @pl.when((i >= 0) & (i < 4))
        def _():
            lj = (j // 32) * 2 + j % 2
            for m in range(4):
                @pl.when(lj // 8 == m)
                def _():
                    quarters[m][lj % 8] = tiles[s]

            @pl.when(lj < 2)
            def _():
                for m in range(4):
                    quarters[m][8 + lj] = tiles[s]


def extract_columns(pos_t, tiles):
    return pl.pallas_call(
        extract_columns_kernel,
        out_shape=jax.ShapeDtypeStruct((2 * ROWS, T, T), BF),
        in_specs=[SM, VM],
        out_specs=VM,
        compiler_params=pltpu.CompilerParams(vmem_limit_bytes=16 << 20),
        name="extract_columns",
    )(pos_t, tiles)


def extract_rows(pos_t, tiles, after):
    return pl.pallas_call(
        extract_rows_kernel,
        out_shape=[jax.ShapeDtypeStruct((COLS // 4 + 2, T, T), BF)] * 4,
        in_specs=[SM, VM, pl.BlockSpec(memory_space=pl.ANY)],
        out_specs=[VM] * 4,
        compiler_params=pltpu.CompilerParams(vmem_limit_bytes=16 << 20),
        name="extract_rows",
    )(pos_t, tiles, after)


def dot(a, b):
    return jnp.dot(a, b, preferred_element_type=F32)


def update_kernel(
    pos, me, tiles, pivots, inverses, panel0, b0, b1, b2, b3, rows_mine, rows_other, corner_other,
    out, lc, uc,
):
    p, q = me[0], me[1]
    c = p % 2
    my_x, my_y = q // 4, q % 4
    w0 = inverses[0]
    w1 = inverses[1]

    place = lax.broadcasted_iota(jnp.int32, (256, 256), 0)
    place = jnp.where(place < 128, place + c * 128, place - c * 128)

    def permutation(k):
        hot = (jnp.broadcast_to(pivots[k : k + 1, :], (256, 256)) == place).astype(F32)
        return hot.T.astype(BF)

    perm0 = permutation(0)
    perm1 = permutation(1)

    def pair(mine, m, other, o):
        top = jnp.concatenate([mine[m], mine[m + 1]], axis=1)
        low = jnp.concatenate([other[o], other[o + 1]], axis=1)
        return jnp.concatenate([top, low], axis=0)

    low_rows = dot(pair(panel0, 16, corner_other, 0), w0).astype(BF)
    corner = dot(perm0, pair(panel0, 34, corner_other, 2)).astype(BF)

    @pl.loop(0, 4)
    def _(m):
        def rows(base):
            return jnp.concatenate(
                [pair(rows_mine, base + 2 * h, rows_other, base + 2 * h) for h in range(4)], axis=1
            )

        first = dot(perm0, rows(m * 16)).astype(BF)
        new = (rows(m * 16 + 8).astype(F32) - dot(low_rows, first)).astype(BF)
        head = jnp.where((m == 0) & (q == 0), low_rows, new[:, :256])
        second = dot(perm1, jnp.concatenate([head, new[:, 256:]], axis=1)).astype(BF)
        for t in range(8):
            uc[8 * m + t, :256] = first[:, 128 * t : 128 * t + 128]
            uc[8 * m + t, 256:] = second[:, 128 * t : 128 * t + 128]

    def blocks(ref, base):
        rows = [
            jnp.concatenate([ref[base + 2 * g], ref[base + 2 * g + 1]], axis=1) for g in range(8)
        ]
        return jnp.concatenate(rows, axis=0)

    shifts = (0, 3, 1, 2)

    @pl.loop(0, 4)
    def _(y):
        low = dot(blocks(panel0, y * 18), w0).astype(BF)
        for g, dx in enumerate(shifts):
            row = 2 * ((my_x + dx) % 4 * 4 + y)
            lc[row, :, :256] = low[g * 256 : g * 256 + 128]
            lc[row + 1, :, :256] = low[g * 256 + 128 : g * 256 + 256]

    for ref, dx in zip((b0, b1, b2, b3), shifts):
        row_of = [2 * ((my_x + dx) % 4 * 4 + (my_y + dy) % 4) for dy in shifts]
        left = jnp.concatenate([lc[r + h, :, :256] for r in row_of for h in range(2)], axis=0)
        new = (blocks(ref, 0).astype(F32) - dot(left, corner)).astype(BF)
        low = dot(new, w1).astype(BF)
        for g, r in enumerate(row_of):
            lc[r, :, 256:] = low[g * 256 : g * 256 + 128]
            lc[r + 1, :, 256:] = low[g * 256 + 128 : g * 256 + 256]

    def place_of(s):
        i = pos[0, s]
        j = pos[1, s]
        li = jnp.clip(i // 16, 0, ROWS - 1)
        lj = jnp.clip((j // 32) * 2 + j % 2, 0, COLS - 1)
        return i, j, li, lj

    def finish(s):
        i, j, li, lj = place_of(s)

        @pl.when(i < 0)
        def _():
            out[s] = tiles[s]

        @pl.when((i >= 0) & (i < 4))
        def _():
            start = pl.multiple_of((i // 2) * 256 + c * 128, 128)
            out[s] = uc[lj, pl.ds(start, 128), :]

        for t in range(4):
            @pl.when((i >= 4) & (j == t))
            def _():
                out[s] = lc[li, :, t * 128 : t * 128 + 128]

    @pl.loop(0, SLOTS // 8)
    def _(b):
        least = jnp.int32(4)
        for k in range(8):
            s = b * 8 + k
            i, j, li, lj = place_of(s)
            least = jnp.minimum(least, jnp.minimum(i, j))
            out[s] = (tiles[s].astype(F32) - dot(lc[li], uc[lj])).astype(BF)

        @pl.when(least < 4)
        def _():
            @pl.loop(b * 8, b * 8 + 8)
            def _(s):
                finish(s)


def update(*args):
    return pl.pallas_call(
        update_kernel,
        out_shape=jax.ShapeDtypeStruct((SLOTS, T, T), BF),
        in_specs=[SM, SM] + [VM] * (len(args) - 2),
        out_specs=VM,
        scratch_shapes=[
            pltpu.VMEM((ROWS, T, 4 * T), BF),
            pltpu.VMEM((COLS, 4 * T, T), BF),
        ],
        compiler_params=pltpu.CompilerParams(vmem_limit_bytes=48 << 20),
        name="update",
    )(*args)


def spread(piece, groups):
    copies = jnp.broadcast_to(piece[None], (4,) + piece.shape).reshape(-1, T, T)
    return lax.all_to_all(copies, "pcol", 0, 0, tiled=True, axis_index_groups=groups)


def around(piece, move):
    return [piece] + [lax.ppermute(piece, "pcol", move(d)) for d in (1, -1, 2)]


def local(tiles, tile_pos, pivots, inverses):
    p = lax.axis_index("prow")
    q = lax.axis_index("pcol")
    pos_t = tile_pos.T
    me = jnp.stack([p, q]).astype(jnp.int32)
    col = extract_columns(pos_t, tiles)
    quarters = extract_rows(pos_t, tiles, col)

    with jax.named_scope("row_scatter"):
        quarter = quarters[0]
        for m in range(1, 4):
            got = lax.ppermute(quarters[m], "prow", scatter_z(m))
            quarter = jnp.where(p // 4 == m, got, quarter)
    with jax.named_scope("column_scatter"):
        shards = lax.all_to_all(col, "pcol", 0, 0, tiled=True)
    with jax.named_scope("row_gather"):
        rows_mine = lax.all_gather(
            quarter[:8], "prow", tiled=True, axis_index_groups=SAME_CORE
        )
    with jax.named_scope("corner_gather"):
        held, shards = lax.optimization_barrier((quarter[8:], shards))
        below = lax.ppermute(held, "prow", UP_Z)
        corner = jnp.where((p // 2 + q) % 2 == 1, held, below)
    with jax.named_scope("column_gather"):
        first0 = around(jnp.concatenate([shards[:4], corner]), move_x)
        first1 = jnp.concatenate(around(shards[4:8], move_y))
        x = q // 4
        corner = first0[0][4:]
        for k, g in ((1, 1), (2, 3), (3, 2)):
            corner = jnp.where(x == k, first0[g][4:], corner)
        join0 = [g[:4] for g in first0] + [corner]
        panel0 = spread(jnp.concatenate(join0), ALONG_Y)
        panel1 = around(first1, move_x)
    with jax.named_scope("core_swap"):
        late, _ = lax.optimization_barrier((rows_mine, first1))
        rows_other = lax.ppermute(late, "prow", SWAP)
        corner_other = lax.ppermute(jnp.concatenate([panel0[16:18], panel0[34:36]]), "prow", SWAP)
    return update(
        pos_t, me, tiles, pivots, inverses, panel0, *panel1, rows_mine, rows_other, corner_other
    )


def solution(mesh):
    return jax.shard_map(
        local,
        mesh=mesh,
        in_specs=(P(("prow", "pcol"), None, None), P(("prow", "pcol"), None), P(), P()),
        out_specs=P(("prow", "pcol"), None, None),
        check_vma=False,
    )
```

```python
import jax
import jax.numpy as jnp
from jax import lax
from jax.experimental import pallas as pl
from jax.experimental.pallas import tpu as pltpu
from jax.sharding import PartitionSpec as P

T = 128
BF = jnp.bfloat16
F32 = jnp.float32
SLOTS = 128
ROWS = 32
COLS = 32
PARTS = 4


ALONG_Y = [[x * 4 + y for y in range(4)] for x in range(4)]
SAME_CORE = [[z * 2 + c for z in range(8)] for c in range(2)]
SWAP = [(p, p ^ 1) for p in range(16)]
ALONG_X = [[x * 4 + y for x in range(4)] for y in range(4)]
UP_Z = [(p, (p + 2) % 16) for p in range(16)]
UP_Z_SWAP = [(p, (p + 2) % 16 ^ 1) for p in range(16)]


def move_x(d):
    return [(x * 4 + y, (x + d) % 4 * 4 + y) for x in range(4) for y in range(4)]


def move_y(d):
    return [(x * 4 + y, x * 4 + (y + d) % 4) for x in range(4) for y in range(4)]


def scatter_z(m):
    return [(k * 2 + c, (2 * m + k) * 2 + c) for k in range(2) for c in range(2)]


VM = pl.BlockSpec(memory_space=pltpu.VMEM)
SM = pl.BlockSpec(memory_space=pltpu.SMEM)
ANY = pl.BlockSpec(memory_space=pl.ANY)
HBM = pl.BlockSpec(memory_space=pltpu.HBM)


def extract_columns_kernel(pos, tiles, after, col):
    @pl.loop(0, SLOTS)
    def _(s):
        i = pos[0, s]
        j = pos[1, s]

        @pl.when((j >= 0) & (j < 4))
        def _():
            col[(i // 16) * 2 + j % 2] = tiles[s]


def extract_rows_kernel(pos, tiles, *quarters):
    @pl.loop(0, SLOTS)
    def _(s):
        i = pos[0, s]
        j = pos[1, s]

        @pl.when((i >= 0) & (i < 4))
        def _():
            lj = (j // 32) * 2 + j % 2
            for m in range(4):
                @pl.when(lj // 8 == m)
                def _():
                    quarters[m][lj % 8] = tiles[s]

            @pl.when(lj < 2)
            def _():
                for m in range(4):
                    quarters[m][8 + lj] = tiles[s]


def extract_columns(pos_t, tiles, after):
    return pl.pallas_call(
        extract_columns_kernel,
        out_shape=jax.ShapeDtypeStruct((2 * ROWS, T, T), BF),
        in_specs=[SM, VM, ANY],
        out_specs=VM,
        compiler_params=pltpu.CompilerParams(vmem_limit_bytes=16 << 20),
        name="extract_columns",
    )(pos_t, tiles, after)


def extract_rows(pos_t, tiles):
    return pl.pallas_call(
        extract_rows_kernel,
        out_shape=[jax.ShapeDtypeStruct((COLS // 4 + 2, T, T), BF)] * 4,
        in_specs=[SM, VM],
        out_specs=[VM] * 4,
        compiler_params=pltpu.CompilerParams(vmem_limit_bytes=16 << 20),
        name="extract_rows",
    )(pos_t, tiles)


def dot(a, b):
    return jnp.dot(a, b, preferred_element_type=F32)


def update_kernel(pos, me, pivots, inverses, *refs):
    sources, out_hbm = refs[:8], refs[8]
    held, (out, lc, uc, in_sem, out_sem) = refs[9:17], refs[17:]
    fetches = [
        pltpu.make_async_copy(a, b, in_sem.at[n]) for n, (a, b) in enumerate(zip(sources, held))
    ]
    for fetch in fetches:
        fetch.start()
    panel0, rows_mine, rows_other, *panel1, tiles = held
    p, q = me[0], me[1]
    c = p % 2
    my_x, my_y = q // 4, q % 4
    w0 = inverses[0]
    w1 = inverses[1]

    place = lax.broadcasted_iota(jnp.int32, (256, 256), 0)
    place = jnp.where(place < 128, place + c * 128, place - c * 128)

    def permutation(k):
        hot = (jnp.broadcast_to(pivots[k : k + 1, :], (256, 256)) == place).astype(F32)
        return hot.T.astype(BF)

    perm0 = permutation(0)
    perm1 = permutation(1)

    def pair(mine, m, other, o):
        top = jnp.concatenate([mine[m], mine[m + 1]], axis=1)
        low = jnp.concatenate([other[o], other[o + 1]], axis=1)
        return jnp.concatenate([top, low], axis=0)

    fetches[0].wait()
    low_rows = dot(pair(panel0, 16, panel0, 18), w0).astype(BF)
    corner = dot(perm0, pair(panel0, 36, panel0, 38)).astype(BF)

    def blocks(ref, base):
        rows = [
            jnp.concatenate([ref[base + 2 * g], ref[base + 2 * g + 1]], axis=1) for g in range(8)
        ]
        return jnp.concatenate(rows, axis=0)

    @pl.loop(0, 4)
    def _(y):
        low = dot(blocks(panel0, y * 20), w0).astype(BF)
        for g in range(4):
            row = 2 * (g * 4 + y)
            lc[row, :, :256] = low[g * 256 : g * 256 + 128]
            lc[row + 1, :, :256] = low[g * 256 + 128 : g * 256 + 256]

    fetches[1].wait()
    fetches[2].wait()

    @pl.loop(0, 4)
    def _(m):
        def rows(base):
            return jnp.concatenate(
                [pair(rows_mine, base + 2 * h, rows_other, base + 2 * h) for h in range(4)], axis=1
            )

        first = dot(perm0, rows(m * 16)).astype(BF)
        new = (rows(m * 16 + 8).astype(F32) - dot(low_rows, first)).astype(BF)
        head = jnp.where((m == 0) & (q == 0), low_rows, new[:, :256])
        second = dot(perm1, jnp.concatenate([head, new[:, 256:]], axis=1)).astype(BF)
        for t in range(8):
            uc[8 * m + t, :256] = first[:, 128 * t : 128 * t + 128]
            uc[8 * m + t, 256:] = second[:, 128 * t : 128 * t + 128]

    shifts = (0, 3, 1, 2)
    for n, (ref, dx) in enumerate(zip(panel1, shifts)):
        fetches[3 + n].wait()
        row_of = [2 * ((my_x + dx) % 4 * 4 + (my_y + dy) % 4) for dy in shifts]
        left = jnp.concatenate([lc[r + h, :, :256] for r in row_of for h in range(2)], axis=0)
        new = (blocks(ref, 0).astype(F32) - dot(left, corner)).astype(BF)
        low = dot(new, w1).astype(BF)
        for g, r in enumerate(row_of):
            lc[r, :, 256:] = low[g * 256 : g * 256 + 128]
            lc[r + 1, :, 256:] = low[g * 256 + 128 : g * 256 + 256]

    def place_of(s):
        i = pos[0, s]
        j = pos[1, s]
        li = jnp.clip(i // 16, 0, ROWS - 1)
        lj = jnp.clip((j // 32) * 2 + j % 2, 0, COLS - 1)
        return i, j, li, lj

    def finish(s):
        i, j, li, lj = place_of(s)

        @pl.when(i < 0)
        def _():
            out[s] = tiles[s]

        @pl.when((i >= 0) & (i < 4))
        def _():
            start = pl.multiple_of((i // 2) * 256 + c * 128, 128)
            out[s] = uc[lj, pl.ds(start, 128), :]

        @pl.when((i >= 4) & (j < 4))
        def _():
            start = pl.multiple_of(j * 128, 128)
            out[s] = lc[li, :, pl.ds(start, 128)]

    fetches[7].wait()
    part = SLOTS // PARTS
    stores = []
    for n in range(PARTS):
        @pl.loop(n * part // 8, (n + 1) * part // 8)
        def _(b):
            least = jnp.int32(4)
            for k in range(8):
                s = b * 8 + k
                i, j, li, lj = place_of(s)
                least = jnp.minimum(least, jnp.minimum(i, j))
                out[s] = (tiles[s].astype(F32) - dot(lc[li], uc[lj])).astype(BF)

            @pl.when(least < 4)
            def _():
                @pl.loop(b * 8, b * 8 + 8)
                def _(s):
                    finish(s)

        span = pl.ds(n * part, part)
        store = pltpu.make_async_copy(out.at[span], out_hbm.at[span], out_sem.at[n])
        store.start()
        stores.append(store)
    for store in stores:
        store.wait()


def update(pos_t, me, pivots, inverses, *arrays):
    return pl.pallas_call(
        update_kernel,
        out_shape=jax.ShapeDtypeStruct((SLOTS, T, T), BF),
        in_specs=[SM, SM, VM, VM] + [HBM] * len(arrays),
        out_specs=HBM,
        scratch_shapes=[pltpu.VMEM(a.shape, BF) for a in arrays]
        + [
            pltpu.VMEM((SLOTS, T, T), BF),
            pltpu.VMEM((ROWS, T, 4 * T), BF),
            pltpu.VMEM((COLS, 4 * T, T), BF),
            pltpu.SemaphoreType.DMA((len(arrays),)),
            pltpu.SemaphoreType.DMA((PARTS,)),
        ],
        compiler_params=pltpu.CompilerParams(vmem_limit_bytes=62 << 20),
        name="update",
    )(pos_t, me, pivots, inverses, *arrays)


def spread(piece, groups):
    copies = jnp.broadcast_to(piece[None], (4,) + piece.shape).reshape(-1, T, T)
    return lax.all_to_all(copies, "pcol", 0, 0, tiled=True, axis_index_groups=groups)


def around(piece, move):
    return [piece] + [lax.ppermute(piece, "pcol", move(d)) for d in (1, -1, 2)]


def local(tiles, tile_pos, pivots, inverses):
    p = lax.axis_index("prow")
    q = lax.axis_index("pcol")
    pos_t = tile_pos.T
    me = jnp.stack([p, q]).astype(jnp.int32)
    quarters = extract_rows(pos_t, tiles)
    col = extract_columns(pos_t, tiles, quarters[0])

    with jax.named_scope("row_scatter"):
        quarter = quarters[0]
        for m in range(1, 4):
            got = lax.ppermute(quarters[m], "prow", scatter_z(m))
            quarter = jnp.where(p // 4 == m, got, quarter)
    with jax.named_scope("column_scatter"):
        shards = lax.all_to_all(col, "pcol", 0, 0, tiled=True)
    with jax.named_scope("row_gather"):
        rows_mine = lax.all_gather(
            quarter[:8], "prow", tiled=True, axis_index_groups=SAME_CORE
        )
    with jax.named_scope("corner_gather"):
        held = quarter[8:]
        below = lax.ppermute(held, "prow", UP_Z)
        below_other = lax.ppermute(held, "prow", UP_Z_SWAP)
        held_other = lax.ppermute(held, "prow", SWAP)
        here = (p // 2 + q) % 2 == 1
        corner = jnp.concatenate(
            [jnp.where(here, held, below), jnp.where(here, held_other, below_other)]
        )
    with jax.named_scope("column_gather"):
        first0 = spread(jnp.concatenate([shards[:4], corner]), ALONG_X)
        first1 = jnp.concatenate(around(shards[4:8], move_y))
        first0, first1 = lax.optimization_barrier((first0, first1))
        join0 = [first0[8 * x : 8 * x + 4] for x in range(4)] + [first0[4:8]]
        panel0 = spread(jnp.concatenate(join0), ALONG_Y)
        panel1 = around(first1, move_x)
    with jax.named_scope("core_swap"):
        late, _, _ = lax.optimization_barrier((rows_mine, panel0, panel1))
        rows_other = lax.ppermute(late, "prow", SWAP)
    return update(
        pos_t, me, pivots, inverses, panel0, rows_mine, rows_other, *panel1, tiles
    )


def solution(mesh):
    return jax.shard_map(
        local,
        mesh=mesh,
        in_specs=(P(("prow", "pcol"), None, None), P(("prow", "pcol"), None), P(), P()),
        out_specs=P(("prow", "pcol"), None, None),
        check_vma=False,
    )
```

```python
import jax
import jax.numpy as jnp
from jax import lax
from jax.experimental import pallas as pl
from jax.experimental.pallas import tpu as pltpu
from jax.sharding import PartitionSpec as P

T = 128
BF = jnp.bfloat16
F32 = jnp.float32
SLOTS = 128
ROWS = 32
COLS = 32
PARTS = 4


ALONG_Y = [[x * 4 + y for y in range(4)] for x in range(4)]
SAME_CORE = [[z * 2 + c for z in range(8)] for c in range(2)]
SWAP = [(p, p ^ 1) for p in range(16)]
ALONG_X = [[x * 4 + y for x in range(4)] for y in range(4)]
UP_Z = [(p, (p + 2) % 16) for p in range(16)]


def move_x(d):
    return [(x * 4 + y, (x + d) % 4 * 4 + y) for x in range(4) for y in range(4)]


def move_y(d):
    return [(x * 4 + y, x * 4 + (y + d) % 4) for x in range(4) for y in range(4)]


def scatter_z(m):
    return [(k * 2 + c, (2 * m + k) * 2 + c) for k in range(2) for c in range(2)]


VM = pl.BlockSpec(memory_space=pltpu.VMEM)
SM = pl.BlockSpec(memory_space=pltpu.SMEM)
ANY = pl.BlockSpec(memory_space=pl.ANY)
HBM = pl.BlockSpec(memory_space=pltpu.HBM)


def extract_columns_kernel(pos, tiles, after, col):
    @pl.loop(0, SLOTS)
    def _(s):
        i = pos[0, s]
        j = pos[1, s]

        @pl.when((j >= 0) & (j < 4))
        def _():
            col[(i // 16) * 2 + j % 2] = tiles[s]


def extract_rows_kernel(pos, tiles, *quarters):
    @pl.loop(0, SLOTS)
    def _(s):
        i = pos[0, s]
        j = pos[1, s]

        @pl.when((i >= 0) & (i < 4))
        def _():
            lj = (j // 32) * 2 + j % 2
            for m in range(4):
                @pl.when(lj // 8 == m)
                def _():
                    quarters[m][lj % 8] = tiles[s]

            @pl.when(lj < 2)
            def _():
                for m in range(4):
                    quarters[m][8 + lj] = tiles[s]


def extract_columns(pos_t, tiles, after):
    return pl.pallas_call(
        extract_columns_kernel,
        out_shape=jax.ShapeDtypeStruct((2 * ROWS, T, T), BF),
        in_specs=[SM, VM, ANY],
        out_specs=VM,
        compiler_params=pltpu.CompilerParams(vmem_limit_bytes=16 << 20),
        name="extract_columns",
    )(pos_t, tiles, after)


def extract_rows(pos_t, tiles):
    return pl.pallas_call(
        extract_rows_kernel,
        out_shape=[jax.ShapeDtypeStruct((COLS // 4 + 2, T, T), BF)] * 4,
        in_specs=[SM, VM],
        out_specs=[VM] * 4,
        compiler_params=pltpu.CompilerParams(vmem_limit_bytes=16 << 20),
        name="extract_rows",
    )(pos_t, tiles)


def dot(a, b):
    return jnp.dot(a, b, preferred_element_type=F32)


def update_kernel(pos, me, pivots, inverses, *refs):
    sources, out_hbm = refs[:9], refs[9]
    held, (out, lc, uc, in_sem, out_sem) = refs[10:19], refs[19:]
    fetches = [
        pltpu.make_async_copy(a, b, in_sem.at[n]) for n, (a, b) in enumerate(zip(sources, held))
    ]
    for fetch in fetches:
        fetch.start()
    panel0, rows_mine, rows_other, *panel1, tiles, corner_other = held
    p, q = me[0], me[1]
    c = p % 2
    my_x, my_y = q // 4, q % 4
    w0 = inverses[0]
    w1 = inverses[1]

    place = lax.broadcasted_iota(jnp.int32, (256, 256), 0)
    place = jnp.where(place < 128, place + c * 128, place - c * 128)

    def permutation(k):
        hot = (jnp.broadcast_to(pivots[k : k + 1, :], (256, 256)) == place).astype(F32)
        return hot.T.astype(BF)

    perm0 = permutation(0)
    perm1 = permutation(1)

    def pair(mine, m, other, o):
        top = jnp.concatenate([mine[m], mine[m + 1]], axis=1)
        low = jnp.concatenate([other[o], other[o + 1]], axis=1)
        return jnp.concatenate([top, low], axis=0)

    fetches[0].wait()
    fetches[8].wait()
    low_rows = dot(pair(panel0, 16, corner_other, 0), w0).astype(BF)
    corner = dot(perm0, pair(panel0, 34, corner_other, 2)).astype(BF)

    def blocks(ref, base):
        rows = [
            jnp.concatenate([ref[base + 2 * g], ref[base + 2 * g + 1]], axis=1) for g in range(8)
        ]
        return jnp.concatenate(rows, axis=0)

    @pl.loop(0, 4)
    def _(y):
        low = dot(blocks(panel0, y * 18), w0).astype(BF)
        for g in range(4):
            row = 2 * (g * 4 + y)
            lc[row, :, :256] = low[g * 256 : g * 256 + 128]
            lc[row + 1, :, :256] = low[g * 256 + 128 : g * 256 + 256]

    fetches[1].wait()
    fetches[2].wait()

    @pl.loop(0, 4)
    def _(m):
        def rows(base):
            return jnp.concatenate(
                [pair(rows_mine, base + 2 * h, rows_other, base + 2 * h) for h in range(4)], axis=1
            )

        first = dot(perm0, rows(m * 16)).astype(BF)
        new = (rows(m * 16 + 8).astype(F32) - dot(low_rows, first)).astype(BF)
        head = jnp.where((m == 0) & (q == 0), low_rows, new[:, :256])
        second = dot(perm1, jnp.concatenate([head, new[:, 256:]], axis=1)).astype(BF)
        for t in range(8):
            uc[8 * m + t, :256] = first[:, 128 * t : 128 * t + 128]
            uc[8 * m + t, 256:] = second[:, 128 * t : 128 * t + 128]

    shifts = (0, 3, 1, 2)
    for n, (ref, dx) in enumerate(zip(panel1, shifts)):
        fetches[3 + n].wait()
        row_of = [2 * ((my_x + dx) % 4 * 4 + (my_y + dy) % 4) for dy in shifts]
        left = jnp.concatenate([lc[r + h, :, :256] for r in row_of for h in range(2)], axis=0)
        new = (blocks(ref, 0).astype(F32) - dot(left, corner)).astype(BF)
        low = dot(new, w1).astype(BF)
        for g, r in enumerate(row_of):
            lc[r, :, 256:] = low[g * 256 : g * 256 + 128]
            lc[r + 1, :, 256:] = low[g * 256 + 128 : g * 256 + 256]

    def place_of(s):
        i = pos[0, s]
        j = pos[1, s]
        li = jnp.clip(i // 16, 0, ROWS - 1)
        lj = jnp.clip((j // 32) * 2 + j % 2, 0, COLS - 1)
        return i, j, li, lj

    def finish(s):
        i, j, li, lj = place_of(s)

        @pl.when(i < 0)
        def _():
            out[s] = tiles[s]

        @pl.when((i >= 0) & (i < 4))
        def _():
            start = pl.multiple_of((i // 2) * 256 + c * 128, 128)
            out[s] = uc[lj, pl.ds(start, 128), :]

        @pl.when((i >= 4) & (j < 4))
        def _():
            start = pl.multiple_of(j * 128, 128)
            out[s] = lc[li, :, pl.ds(start, 128)]

    fetches[7].wait()
    part = SLOTS // PARTS
    stores = []
    for n in range(PARTS):
        @pl.loop(n * part // 8, (n + 1) * part // 8)
        def _(b):
            least = jnp.int32(4)
            for k in range(8):
                s = b * 8 + k
                i, j, li, lj = place_of(s)
                least = jnp.minimum(least, jnp.minimum(i, j))
                out[s] = (tiles[s].astype(F32) - dot(lc[li], uc[lj])).astype(BF)

            @pl.when(least < 4)
            def _():
                @pl.loop(b * 8, b * 8 + 8)
                def _(s):
                    finish(s)

        span = pl.ds(n * part, part)
        store = pltpu.make_async_copy(out.at[span], out_hbm.at[span], out_sem.at[n])
        store.start()
        stores.append(store)
    for store in stores:
        store.wait()


def update(pos_t, me, pivots, inverses, *arrays):
    return pl.pallas_call(
        update_kernel,
        out_shape=jax.ShapeDtypeStruct((SLOTS, T, T), BF),
        in_specs=[SM, SM, VM, VM] + [HBM] * len(arrays),
        out_specs=HBM,
        scratch_shapes=[pltpu.VMEM(a.shape, BF) for a in arrays]
        + [
            pltpu.VMEM((SLOTS, T, T), BF),
            pltpu.VMEM((ROWS, T, 4 * T), BF),
            pltpu.VMEM((COLS, 4 * T, T), BF),
            pltpu.SemaphoreType.DMA((len(arrays),)),
            pltpu.SemaphoreType.DMA((PARTS,)),
        ],
        compiler_params=pltpu.CompilerParams(vmem_limit_bytes=62 << 20),
        name="update",
    )(pos_t, me, pivots, inverses, *arrays)


def spread(piece, groups):
    copies = jnp.broadcast_to(piece[None], (4,) + piece.shape).reshape(-1, T, T)
    return lax.all_to_all(copies, "pcol", 0, 0, tiled=True, axis_index_groups=groups)


def around(piece, move):
    return [piece] + [lax.ppermute(piece, "pcol", move(d)) for d in (1, -1, 2)]


def local(tiles, tile_pos, pivots, inverses):
    p = lax.axis_index("prow")
    q = lax.axis_index("pcol")
    pos_t = tile_pos.T
    me = jnp.stack([p, q]).astype(jnp.int32)
    quarters = extract_rows(pos_t, tiles)
    col = extract_columns(pos_t, tiles, quarters[0])

    with jax.named_scope("row_scatter"):
        quarter = quarters[0]
        for m in range(1, 4):
            got = lax.ppermute(quarters[m], "prow", scatter_z(m))
            quarter = jnp.where(p // 4 == m, got, quarter)
    with jax.named_scope("column_scatter"):
        shards = lax.all_to_all(col, "pcol", 0, 0, tiled=True)
    with jax.named_scope("row_gather"):
        rows_mine = lax.all_gather(
            quarter[:8], "prow", tiled=True, axis_index_groups=SAME_CORE
        )
    with jax.named_scope("corner_gather"):
        held = quarter[8:]
        below = lax.ppermute(held, "prow", UP_Z)
        corner = jnp.where((p // 2 + q) % 2 == 1, held, below)
    with jax.named_scope("column_gather"):
        first0 = spread(jnp.concatenate([shards[:4], corner]), ALONG_X)
        first1 = jnp.concatenate(around(shards[4:8], move_y))
        first0, first1 = lax.optimization_barrier((first0, first1))
        join0 = [first0[6 * x : 6 * x + 4] for x in range(4)] + [first0[4:6]]
        panel0 = spread(jnp.concatenate(join0), ALONG_Y)
        panel1 = around(first1, move_x)
    with jax.named_scope("core_swap"):
        late, _ = lax.optimization_barrier((rows_mine, panel1))
        rows_other = lax.ppermute(late, "prow", SWAP)
        corner_other = lax.ppermute(
            jnp.concatenate([panel0[16:18], panel0[34:36]]), "prow", SWAP
        )
    return update(
        pos_t, me, pivots, inverses, panel0, rows_mine, rows_other, *panel1, tiles, corner_other
    )


def solution(mesh):
    return jax.shard_map(
        local,
        mesh=mesh,
        in_specs=(P(("prow", "pcol"), None, None), P(("prow", "pcol"), None), P(), P()),
        out_specs=P(("prow", "pcol"), None, None),
        check_vma=False,
    )
```

```python
import jax
import jax.numpy as jnp
from jax import lax
from jax.experimental import pallas as pl
from jax.experimental.pallas import tpu as pltpu
from jax.sharding import PartitionSpec as P

T = 128
BF = jnp.bfloat16
F32 = jnp.float32
SLOTS = 128
ROWS = 32
COLS = 32
PARTS = 4


ALONG_Y = [[x * 4 + y for y in range(4)] for x in range(4)]
SAME_CORE = [[z * 2 + c for z in range(8)] for c in range(2)]
SWAP = [(p, p ^ 1) for p in range(16)]
ALONG_X = [[x * 4 + y for x in range(4)] for y in range(4)]
UP_Z = [(p, (p + 2) % 16) for p in range(16)]


def move_x(d):
    return [(x * 4 + y, (x + d) % 4 * 4 + y) for x in range(4) for y in range(4)]


def move_y(d):
    return [(x * 4 + y, x * 4 + (y + d) % 4) for x in range(4) for y in range(4)]


def scatter_z(m):
    return [(k * 2 + c, (2 * m + k) * 2 + c) for k in range(2) for c in range(2)]


VM = pl.BlockSpec(memory_space=pltpu.VMEM)
SM = pl.BlockSpec(memory_space=pltpu.SMEM)
ANY = pl.BlockSpec(memory_space=pl.ANY)
HBM = pl.BlockSpec(memory_space=pltpu.HBM)


def extract_columns_kernel(pos, tiles, after, col):
    @pl.loop(0, SLOTS)
    def _(s):
        i = pos[0, s]
        j = pos[1, s]

        @pl.when((j >= 0) & (j < 4))
        def _():
            col[(i // 16) * 2 + j % 2] = tiles[s]


def extract_rows_kernel(pos, tiles, *quarters):
    @pl.loop(0, SLOTS)
    def _(s):
        i = pos[0, s]
        j = pos[1, s]

        @pl.when((i >= 0) & (i < 4))
        def _():
            lj = (j // 32) * 2 + j % 2
            for m in range(4):
                @pl.when(lj // 8 == m)
                def _():
                    quarters[m][lj % 8] = tiles[s]

            @pl.when(lj < 2)
            def _():
                for m in range(4):
                    quarters[m][8 + lj] = tiles[s]


def extract_columns(pos_t, tiles, after):
    return pl.pallas_call(
        extract_columns_kernel,
        out_shape=jax.ShapeDtypeStruct((2 * ROWS, T, T), BF),
        in_specs=[SM, VM, ANY],
        out_specs=VM,
        compiler_params=pltpu.CompilerParams(vmem_limit_bytes=16 << 20),
        name="extract_columns",
    )(pos_t, tiles, after)


def extract_rows(pos_t, tiles):
    return pl.pallas_call(
        extract_rows_kernel,
        out_shape=[jax.ShapeDtypeStruct((COLS // 4 + 2, T, T), BF)] * 4,
        in_specs=[SM, VM],
        out_specs=[VM] * 4,
        compiler_params=pltpu.CompilerParams(vmem_limit_bytes=16 << 20),
        name="extract_rows",
    )(pos_t, tiles)


def dot(a, b):
    return jnp.dot(a, b, preferred_element_type=F32)


def update_kernel(pos, me, pivots, inverses, *refs):
    sources, out_hbm = refs[:9], refs[9]
    held, (out, lc, uc, in_sem, out_sem) = refs[10:19], refs[19:]
    fetches = [
        pltpu.make_async_copy(a, b, in_sem.at[n]) for n, (a, b) in enumerate(zip(sources, held))
    ]
    for n in (8, 0, 1, 2, 3, 4, 5, 6, 7):
        fetches[n].start()
    panel0, rows_mine, rows_other, *panel1, tiles, corner_other = held
    p, q = me[0], me[1]
    c = p % 2
    my_x, my_y = q // 4, q % 4
    w0 = inverses[0]
    w1 = inverses[1]

    place = lax.broadcasted_iota(jnp.int32, (256, 256), 0)
    place = jnp.where(place < 128, place + c * 128, place - c * 128)

    def permutation(k):
        hot = (jnp.broadcast_to(pivots[k : k + 1, :], (256, 256)) == place).astype(F32)
        return hot.T.astype(BF)

    perm0 = permutation(0)
    perm1 = permutation(1)

    def pair(mine, m, other, o):
        top = jnp.concatenate([mine[m], mine[m + 1]], axis=1)
        low = jnp.concatenate([other[o], other[o + 1]], axis=1)
        return jnp.concatenate([top, low], axis=0)

    fetches[0].wait()
    fetches[8].wait()
    low_rows = dot(pair(panel0, 16, corner_other, 0), w0).astype(BF)
    corner = dot(perm0, pair(panel0, 34, corner_other, 2)).astype(BF)

    def blocks(ref, base):
        rows = [
            jnp.concatenate([ref[base + 2 * g], ref[base + 2 * g + 1]], axis=1) for g in range(8)
        ]
        return jnp.concatenate(rows, axis=0)

    @pl.loop(0, 4)
    def _(y):
        low = dot(blocks(panel0, y * 18), w0).astype(BF)
        for g in range(4):
            row = 2 * (g * 4 + y)
            lc[row, :, :256] = low[g * 256 : g * 256 + 128]
            lc[row + 1, :, :256] = low[g * 256 + 128 : g * 256 + 256]

    fetches[1].wait()
    fetches[2].wait()

    @pl.loop(0, 4)
    def _(m):
        def rows(base):
            return jnp.concatenate(
                [pair(rows_mine, base + 2 * h, rows_other, base + 2 * h) for h in range(4)], axis=1
            )

        first = dot(perm0, rows(m * 16)).astype(BF)
        new = (rows(m * 16 + 8).astype(F32) - dot(low_rows, first)).astype(BF)
        head = jnp.where((m == 0) & (q == 0), low_rows, new[:, :256])
        second = dot(perm1, jnp.concatenate([head, new[:, 256:]], axis=1)).astype(BF)
        for t in range(8):
            uc[8 * m + t, :256] = first[:, 128 * t : 128 * t + 128]
            uc[8 * m + t, 256:] = second[:, 128 * t : 128 * t + 128]

    shifts = (0, 3, 1, 2)
    for n, (ref, dx) in enumerate(zip(panel1, shifts)):
        fetches[3 + n].wait()
        row_of = [2 * ((my_x + dx) % 4 * 4 + (my_y + dy) % 4) for dy in shifts]
        left = jnp.concatenate([lc[r + h, :, :256] for r in row_of for h in range(2)], axis=0)
        new = (blocks(ref, 0).astype(F32) - dot(left, corner)).astype(BF)
        low = dot(new, w1).astype(BF)
        for g, r in enumerate(row_of):
            lc[r, :, 256:] = low[g * 256 : g * 256 + 128]
            lc[r + 1, :, 256:] = low[g * 256 + 128 : g * 256 + 256]

    def place_of(s):
        i = pos[0, s]
        j = pos[1, s]
        li = jnp.clip(i // 16, 0, ROWS - 1)
        lj = jnp.clip((j // 32) * 2 + j % 2, 0, COLS - 1)
        return i, j, li, lj

    def finish(s):
        i, j, li, lj = place_of(s)

        @pl.when(i < 0)
        def _():
            out[s] = tiles[s]

        @pl.when((i >= 0) & (i < 4))
        def _():
            start = pl.multiple_of((i // 2) * 256 + c * 128, 128)
            out[s] = uc[lj, pl.ds(start, 128), :]

        @pl.when((i >= 4) & (j < 4))
        def _():
            start = pl.multiple_of(j * 128, 128)
            out[s] = lc[li, :, pl.ds(start, 128)]

    fetches[7].wait()
    part = SLOTS // PARTS
    stores = []
    for n in range(PARTS):
        @pl.loop(n * part // 8, (n + 1) * part // 8)
        def _(b):
            least = jnp.int32(4)
            for k in range(8):
                s = b * 8 + k
                i, j, li, lj = place_of(s)
                least = jnp.minimum(least, jnp.minimum(i, j))
                out[s] = (tiles[s].astype(F32) - dot(lc[li], uc[lj])).astype(BF)

            @pl.when(least < 4)
            def _():
                @pl.loop(b * 8, b * 8 + 8)
                def _(s):
                    finish(s)

        span = pl.ds(n * part, part)
        store = pltpu.make_async_copy(out.at[span], out_hbm.at[span], out_sem.at[n])
        store.start()
        stores.append(store)
    for store in stores:
        store.wait()


def update(pos_t, me, pivots, inverses, *arrays):
    return pl.pallas_call(
        update_kernel,
        out_shape=jax.ShapeDtypeStruct((SLOTS, T, T), BF),
        in_specs=[SM, SM, VM, VM] + [HBM] * len(arrays),
        out_specs=HBM,
        scratch_shapes=[pltpu.VMEM(a.shape, BF) for a in arrays]
        + [
            pltpu.VMEM((SLOTS, T, T), BF),
            pltpu.VMEM((ROWS, T, 4 * T), BF),
            pltpu.VMEM((COLS, 4 * T, T), BF),
            pltpu.SemaphoreType.DMA((len(arrays),)),
            pltpu.SemaphoreType.DMA((PARTS,)),
        ],
        compiler_params=pltpu.CompilerParams(vmem_limit_bytes=62 << 20),
        name="update",
    )(pos_t, me, pivots, inverses, *arrays)


def spread(piece, groups):
    copies = jnp.broadcast_to(piece[None], (4,) + piece.shape).reshape(-1, T, T)
    return lax.all_to_all(copies, "pcol", 0, 0, tiled=True, axis_index_groups=groups)


def around(piece, move):
    return [piece] + [lax.ppermute(piece, "pcol", move(d)) for d in (1, -1, 2)]


def local(tiles, tile_pos, pivots, inverses):
    p = lax.axis_index("prow")
    q = lax.axis_index("pcol")
    pos_t = tile_pos.T
    me = jnp.stack([p, q]).astype(jnp.int32)
    quarters = extract_rows(pos_t, tiles)
    col = extract_columns(pos_t, tiles, quarters[0])

    with jax.named_scope("row_scatter"):
        quarter = quarters[0]
        for m in range(1, 4):
            got = lax.ppermute(quarters[m], "prow", scatter_z(m))
            quarter = jnp.where(p // 4 == m, got, quarter)
    with jax.named_scope("column_scatter"):
        shards = lax.all_to_all(col, "pcol", 0, 0, tiled=True)
    with jax.named_scope("row_gather"):
        rows_mine = lax.all_gather(
            quarter[:8], "prow", tiled=True, axis_index_groups=SAME_CORE
        )
    with jax.named_scope("corner_gather"):
        held = quarter[8:]
        below = lax.ppermute(held, "prow", UP_Z)
        corner = jnp.where((p // 2 + q) % 2 == 1, held, below)
    with jax.named_scope("column_gather"):
        first0 = spread(jnp.concatenate([shards[:4], corner]), ALONG_X)
        first1 = jnp.concatenate(around(shards[4:8], move_y))
        first0, first1 = lax.optimization_barrier((first0, first1))
        join0 = [first0[6 * x : 6 * x + 4] for x in range(4)] + [first0[4:6]]
        panel0 = spread(jnp.concatenate(join0), ALONG_Y)
        panel1 = around(first1, move_x)
    with jax.named_scope("core_swap"):
        late, _ = lax.optimization_barrier((rows_mine, panel1))
        rows_other = lax.ppermute(late, "prow", SWAP)
        corner_other = lax.ppermute(
            jnp.concatenate([panel0[16:18], panel0[34:36]]), "prow", SWAP
        )
    return update(
        pos_t, me, pivots, inverses, panel0, rows_mine, rows_other, *panel1, tiles, corner_other
    )


def solution(mesh):
    return jax.shard_map(
        local,
        mesh=mesh,
        in_specs=(P(("prow", "pcol"), None, None), P(("prow", "pcol"), None), P(), P()),
        out_specs=P(("prow", "pcol"), None, None),
        check_vma=False,
    )
```
